32 devices in a mesh: seq: 2 (over y), dom: 8 (over z, x), tm: 2 (over core).
Axes of the slice: x: 2, y: 2, z: 4, core: 2. Of those that a mesh axis runs over, the one named last changes fastest.
Arguments:
- particles: bfloat16 [4, 1536, 128], P('tm', ('seq', 'dom')), parts along dimension 1, may hold values from -6 to 6
- log_weight: float32 [4, 1536], P('tm', ('seq', 'dom')), parts along dimension 1, may hold values from -13 to 313
- trans_weight: bfloat16 [128, 128], replicated, may hold values from -0.5 to 0.5
- precision: float32 [128], replicated, may hold values from 0.2 to 2
Outputs:
- smoothed: float32 [4, 1536], P('tm', ('seq', 'dom')), parts along dimension 1
- score: float32 [256, 128], P('seq'), parts along dimension 0
The draws below stay inside these ranges and needn't reach their ends.
There are 2 independent parts, one for each index of `seq`. The reference program is written for one: setup_inputs(seed, part) draws one part's arguments, and reference() takes and returns one part's arrays. A program takes and returns all parts, laid end to end along the dimension named above; an argument that names none is the same for every part. Nothing has to cross between parts.
All inputs are finite; a program needn't handle non-finite values.
Results may differ from the reference program's by a relative error of at most 0.0061.
Values may be sent and summed in bfloat16 or wider, within the bound.
A program may use at most 64 MiB of HBM per device.

```python
import math
import jax
import jax.numpy as jnp
from jax import lax

D = 128
N_DEV = 96
N = 768
WINDOW = 4
N_DOM = 8


def draw_log_weight(key, part):
    base_key, shift_key = jax.random.split(key)
    base = jax.random.truncated_normal(base_key, -5.0, 5.0, (WINDOW, N), jnp.float32) * 1.5
    offset = jax.random.uniform(shift_key, (WINDOW,), jnp.float32, -4.0, 4.0)
    return base + offset[:, None]


def block_scale(key, extent, cuts, least, top_value):
    def one(position, blocks):
        heights = jax.random.uniform(jax.random.fold_in(jax.random.fold_in(key, 6), position), (blocks,), jnp.float32, least / len(cuts), top_value / len(cuts))
        return jnp.repeat(jnp.exp(heights), extent[position] // blocks).reshape((-1,) + (1,) * (len(extent) - position - 1))

    level = one(*cuts[0])
    for cut in cuts[1:]:
        level = level * one(*cut)
    return level


def gaussian(key, shape, scale, most, shards=(), kind=jnp.bfloat16):
    values = jax.random.normal(key, shape, jnp.float32) * scale
    if len(shards) > 0:
        values = block_scale(key, shape, shards, -0.22, 0.18) * values
    return jnp.clip(values, min=-most, max=most).astype(kind)


def setup_inputs(seed: int = 0, part: int = 0) -> dict:
    keys = jax.random.split(jax.random.key(seed), 5)
    own_keys = jax.random.split(jax.random.fold_in(keys[4], part), 5)
    particles = gaussian(own_keys[0], (WINDOW, N, D), 1.0, 6.0, ((0, 2), (1, 8)))
    log_weight = draw_log_weight(jax.random.fold_in(jax.random.fold_in(keys[4], part), 71), part)
    trans_weight = gaussian(keys[2], (D, D), D ** -0.5, 0.5)
    precision = jnp.clip(jnp.exp(jax.random.uniform(keys[3], (D,), jnp.float32, math.log(0.2), math.log(2.0))), 0.2, 2.0)
    return dict(particles=particles, log_weight=log_weight, trans_weight=trans_weight, precision=precision)


def reference(particles, log_weight, trans_weight, precision):
    exact_mode = lax.Precision.HIGHEST
    weight_full = trans_weight.astype(jnp.float32)
    width = particles.shape[2]
    total_rows = particles.shape[1]
    final_logs = log_weight[WINDOW - 1]
    highest = jnp.max(final_logs)
    expanded = jnp.exp(final_logs - highest)
    smoothed = [None] * WINDOW
    smoothed[WINDOW - 1] = expanded / jnp.sum(expanded)
    score = jnp.zeros((width, width), jnp.float32)
    for t in range(WINDOW - 2, -1, -1):
        columns = particles[t]
        later = particles[t + 1]
        predicted = jnp.dot(columns, trans_weight.T, preferred_element_type=jnp.float32)
        column_bias = log_weight[t] - 0.5 * jnp.sum(precision * predicted * predicted, axis=1)
        projected = jnp.dot(later.astype(jnp.float32) * precision, weight_full, precision=exact_mode).astype(jnp.bfloat16)
        blocks = (projected.reshape(N_DOM, N_DEV, width), smoothed[t + 1].reshape(N_DOM, N_DEV), later.reshape(N_DOM, N_DEV, width))

        def accumulate(carried, block):
            column_sums, outer = carried
            proj_block, weight_block, later_block = block
            scores = jnp.dot(proj_block, columns.T, preferred_element_type=jnp.float32) + column_bias[None, :]
            row_top = jnp.max(scores, axis=1)
            row_norm = row_top + jnp.log(jnp.sum(jnp.exp(scores - row_top[:, None]), axis=1))
            backward = (weight_block[:, None] * jnp.exp(scores - row_norm[:, None])).astype(jnp.bfloat16)
            column_sums = column_sums + jnp.sum(backward.astype(jnp.float32), axis=0)
            moved = jnp.dot(backward, columns, preferred_element_type=jnp.float32)
            outer = outer + jnp.dot(later_block.astype(jnp.float32).T, moved, precision=exact_mode)
            return (column_sums, outer), None

        start_state = (jnp.zeros((total_rows,), jnp.float32), jnp.zeros((width, width), jnp.float32))
        (column_sums, outer), unused = lax.scan(accumulate, start_state, blocks)
        column_float = columns.astype(jnp.float32)
        moment = jnp.dot(column_float.T * column_sums[None, :], column_float, precision=exact_mode)
        score = score + precision[:, None] * (outer - jnp.dot(weight_full, moment, precision=exact_mode))
        smoothed[t] = column_sums
    return jnp.stack(smoothed) * total_rows, score
```

```python
import functools

import jax
import jax.numpy as jnp
from jax import lax
from jax.experimental import pallas as pl
from jax.experimental.pallas import tpu as pltpu
from jax.sharding import PartitionSpec as P

exact_mode = lax.Precision.HIGHEST


def from_behind(x, axis, by):
    size = lax.axis_size(axis)
    pairs = [(i, i + by) for i in range(size) if 0 <= i + by < size]
    return lax.ppermute(x, axis, pairs)


def block_size(length):
    best = 1
    for trial in range(1, min(length, 512) + 1):
        if length % trial == 0:
            best = trial
    return best


def project_rows(rows, precision, weight_full):
    return jnp.dot(rows.astype(jnp.float32) * precision, weight_full, precision=exact_mode).astype(
        jnp.bfloat16
    )


def pair_scores(row_proj, column_rows, column_bias):
    return (
        jnp.einsum("id,jd->ij", row_proj, column_rows, preferred_element_type=jnp.float32)
        + column_bias[None, :]
    )


def make_norm_fold(row_proj, bias_row, carried, block_in, first_row):
    length = block_in.shape[0]
    size = block_size(length)

    def inner(position, state):
        row_top, row_total = state
        offset = position * size
        column_rows = lax.dynamic_slice_in_dim(block_in, offset, size, 0)
        bias_part = lax.dynamic_slice_in_dim(bias_row, first_row + offset, size, 0)
        scores = pair_scores(row_proj, column_rows, bias_part)
        new_top = jnp.maximum(row_top, jnp.max(scores, axis=1))
        row_total = row_total * jnp.exp(row_top - new_top) + jnp.sum(
            jnp.exp(scores - new_top[:, None]), axis=1
        )
        return (new_top, row_total)

    return lax.fori_loop(0, length // size, inner, carried)


def make_column_fold(row_proj, bias_row, row_norm, row_weight, carried, block_in, first_row):
    length = block_in.shape[0]
    size = block_size(length)

    def inner(position, state):
        moved, column_sums = state
        offset = position * size
        column_rows = lax.dynamic_slice_in_dim(block_in, offset, size, 0)
        bias_part = lax.dynamic_slice_in_dim(bias_row, first_row + offset, size, 0)
        scores = pair_scores(row_proj, column_rows, bias_part)
        backward = (row_weight[:, None] * jnp.exp(scores - row_norm[:, None])).astype(jnp.bfloat16)
        moved = moved + jnp.dot(backward, column_rows, preferred_element_type=jnp.float32)
        column_sums = lax.dynamic_update_slice_in_dim(
            column_sums, jnp.sum(backward.astype(jnp.float32), axis=0), first_row + offset, 0
        )
        return (moved, column_sums)

    return lax.fori_loop(0, length // size, inner, carried)


def shards(particles, log_weight, trans_weight, precision):
    steps_here, rows_here, width = particles.shape
    tm_count = lax.axis_size("tm")
    dom_count = lax.axis_size("dom")
    total_rows = rows_here * dom_count
    tm_place = lax.axis_index("tm")
    is_last = tm_place == tm_count - 1
    weight_full = trans_weight.astype(jnp.float32)
    boundary = from_behind(particles[0], "tm", -1)
    later_sets = [particles[1]] + [boundary]
    later_proj = [project_rows(rows, precision, weight_full) for rows in later_sets]
    biases = []
    for k in range(steps_here):
        predicted = jnp.dot(particles[k], trans_weight.T, preferred_element_type=jnp.float32)
        biases.append(log_weight[k] - 0.5 * jnp.sum(precision * predicted * predicted, axis=1))
    local_bias = jnp.stack(biases)
    full_bias = lax.all_gather(local_bias, "dom", axis=1, tiled=True)
    row_norms = []
    whole = lax.all_gather(particles, "dom", axis=1, tiled=True)
    for k in range(steps_here):
        start_state = (
            jnp.full((rows_here,), -jnp.inf, jnp.float32),
            jnp.zeros((rows_here,), jnp.float32),
        )
        row_top, row_total = make_norm_fold(later_proj[k], full_bias[k], start_state, whole[k], 0)
        row_norms.append(row_top + jnp.log(row_total))
    final_logs = log_weight[steps_here - 1]
    global_top = lax.pmax(jnp.max(final_logs), "dom")
    global_total = lax.psum(jnp.sum(jnp.exp(final_logs - global_top)), "dom")
    final_weights = jnp.exp(final_logs - global_top) / global_total
    carried = (
        jnp.zeros((steps_here, rows_here), jnp.float32),
        jnp.zeros((width, width), jnp.float32),
    )
    for r in range(tm_count):
        if r == 0:
            incoming = jnp.zeros((rows_here,), jnp.float32)
        else:
            incoming = from_behind(carried[0][0], "tm", -1)
        owner = tm_count - 1 - r
        backward_partial_value = jnp.zeros((width, width), jnp.float32)
        outputs = [None] * steps_here
        row_weight = incoming
        for backward_k in range(steps_here - 1, -1, -1):
            column_rows = particles[backward_k]
            backward_start_state = (
                jnp.zeros((rows_here, width), jnp.float32),
                jnp.zeros((total_rows,), jnp.float32),
            )
            moved, column_sums = make_column_fold(
                later_proj[backward_k],
                full_bias[backward_k],
                row_norms[backward_k],
                row_weight,
                backward_start_state,
                whole[backward_k],
                0,
            )
            column_weights = lax.psum_scatter(column_sums, "dom", scatter_dimension=0, tiled=True)
            outer = jnp.dot(
                later_sets[backward_k].astype(jnp.float32).T, moved, precision=exact_mode
            )
            column_float = column_rows.astype(jnp.float32)
            moment = jnp.dot(
                column_float.T * column_weights[None, :], column_float, precision=exact_mode
            )
            backward_partial_value = backward_partial_value + precision[:, None] * (
                outer - jnp.dot(weight_full, moment, precision=exact_mode)
            )
            if backward_k == steps_here - 1:
                column_weights = jnp.where(is_last, final_weights, column_weights)
            outputs[backward_k] = column_weights
            row_weight = column_weights
        is_owner = tm_place == owner
        carried = (
            jnp.where(is_owner, jnp.stack(outputs), carried[0]),
            jnp.where(is_owner, backward_partial_value, carried[1]),
        )
    stacked, partial_value = carried
    score = lax.psum(partial_value, ("dom", "tm"))
    return (stacked * total_rows, score)


MESH = pl.DeviceIdType.MESH
EXTRA = 16
MOST_ROWS = 1024


def nt_dot(a, b):
    return lax.dot_general(a, b, (((1,), (1,)), ((), ())), preferred_element_type=jnp.float32)


def tn_dot(a, b):
    return lax.dot_general(a, b, (((0,), (0,)), ((), ())), preferred_element_type=jnp.float32)


def nn_dot(a, b):
    return jnp.dot(a, b, preferred_element_type=jnp.float32)


def split_three(x):
    high = x.astype(jnp.bfloat16)
    rest = x - high.astype(jnp.float32)
    middle = rest.astype(jnp.bfloat16)
    low = (rest - middle.astype(jnp.float32)).astype(jnp.bfloat16)
    return high, middle, low


def smoother_kernel(
    n_dom, x_ref, lw_ref, w_ref, p_ref, smoothed_ref, score_ref,
    held, kernel_rows, inverse_norm, bias, weights, stage, send_sem, recv_sem,
):
    rows, width = x_ref.shape[1:]
    total = n_dom * rows
    steps = 4
    half = total // 2
    dom = lax.axis_index("dom")
    tm = lax.axis_index("tm")
    group, side = dom // 2, dom % 2
    groups = n_dom // 2
    across = dom + 1 - 2 * side
    other = 1 - tm
    mine = tm * n_dom + dom
    peers = [lax.rem(group + k, groups) * 2 + side for k in range(1, groups)]

    barrier = pltpu.get_barrier_semaphore()
    targets = [(peer, tm) for peer in peers] + [(across, tm), (dom, other)]
    for to_dom, to_tm in targets:
        pl.semaphore_signal(
            barrier, inc=1, device_id={"dom": to_dom, "tm": to_tm}, device_id_type=MESH
        )

    weight = w_ref[...]
    p_row = p_ref[...]
    p_down = jnp.broadcast_to(p_row, (width, width)).T
    stage[...] = jnp.zeros_like(stage)
    terms = []
    for k in range(2):
        x_k = x_ref[k]
        held[mine, k * rows : (k + 1) * rows, :] = x_k
        predicted = nt_dot(weight, x_k)
        energy = jnp.sum(p_down[:, :rows] * predicted * predicted, axis=0, keepdims=True)
        terms.append(lw_ref[k : k + 1, :] - 0.5 * energy)
    terms.append(lw_ref[1:2, :])
    for q in range(3):
        for piece, value in enumerate(split_three(terms[q])):
            row = 3 * piece + q
            stage[row : row + 1, 0:rows] = value.astype(jnp.float32)
    held[mine, 2 * rows : 2 * rows + EXTRA, :] = stage[...].astype(jnp.bfloat16)

    pl.semaphore_wait(barrier, len(targets))

    sends = []

    def send(slot, to_dom, to_tm):
        copy = pltpu.make_async_remote_copy(
            src_ref=held.at[slot],
            dst_ref=held.at[slot],
            send_sem=send_sem.at[len(sends)],
            recv_sem=recv_sem.at[slot],
            device_id={"dom": to_dom, "tm": to_tm},
            device_id_type=MESH,
        )
        copy.start()
        sends.append(copy)

    def arrive(slot):
        pltpu.make_async_remote_copy(
            src_ref=held.at[slot],
            dst_ref=held.at[slot],
            send_sem=send_sem.at[0],
            recv_sem=recv_sem.at[slot],
            device_id={"dom": dom, "tm": other},
            device_id_type=MESH,
        ).wait_recv()

    for peer in peers:
        send(mine, peer, tm)
    send(mine, across, tm)
    send(mine, dom, other)

    scaled = jnp.concatenate(
        split_three(p_down * weight.astype(jnp.float32)), axis=1
    )

    for peer in peers:
        slot = tm * n_dom + peer
        arrive(slot)
        send(slot, across, tm)
        send(slot, dom, other)
    for pair in [across] + [peer + 1 - 2 * side for peer in peers]:
        slot = tm * n_dom + pair
        arrive(slot)
        send(slot, dom, other)
    for d in range(n_dom):
        arrive(other * n_dom + d)

    def set_of(t, first=0, count=n_dom):
        at = (t // 2) * n_dom + first
        k = t % 2
        return held[at : at + count, k * rows : (k + 1) * rows, :].reshape(count * rows, width)

    line = lax.broadcasted_iota(jnp.int32, (EXTRA, 3 * width), 0)
    which = lax.broadcasted_iota(jnp.int32, (EXTRA, 3 * width), 1) // width
    pick = jnp.where((line < 9) & (line % 3 == which), 1.0, 0.0).astype(jnp.bfloat16)
    for s in range(2 * n_dom):
        spread = tn_dot(held[s, 2 * rows : 2 * rows + EXTRA, :], pick)
        at = (s % n_dom) * rows
        for k in range(2):
            t = 2 * (s // n_dom) + k
            part = spread[:rows, k * width : (k + 1) * width]
            if t == steps - 1:
                part = spread[:rows, 2 * width :]
            bias[t, at : at + rows, :] = part

    last = bias[steps - 1]
    last = jnp.exp(last - jnp.max(last, axis=0, keepdims=True))
    weights[steps - 1] = last / jnp.sum(last, axis=0, keepdims=True)

    for t in range(steps - 2, -1, -1):
        for h in range(2):
            later = set_of(t + 1, h * (n_dom // 2), n_dom // 2)
            wide = nn_dot(later, scaled)
            projected = (
                wide[:, :width] + (wide[:, width : 2 * width] + wide[:, 2 * width :])
            ).astype(jnp.bfloat16)
            scores = nt_dot(set_of(t), projected)
            scores = scores + jnp.concatenate([bias[t]] * (half // width), axis=1)
            top = jnp.max(scores, axis=0, keepdims=True)
            terms = jnp.exp(scores - top)
            inverse = 1.0 / jnp.sum(terms, axis=0, keepdims=True)
            kernel_rows[t, :, h * half : (h + 1) * half] = terms.astype(jnp.bfloat16)
            for b in range(half // width):
                at = h * half + b * width
                inverse_norm[t, at : at + width, :] = jnp.broadcast_to(
                    inverse[:, b * width : (b + 1) * width], (width, width)
                ).T

    score = jnp.zeros((width, width), jnp.float32)
    for t in range(steps - 2, -1, -1):
        ratio = weights[t + 1] * inverse_norm[t]
        right = jnp.concatenate(
            [(ratio * set_of(t + 1).astype(jnp.float32)).astype(jnp.bfloat16), ratio.astype(jnp.bfloat16)],
            axis=1,
        )
        both = nn_dot(kernel_rows[t], right)
        now = both[:, width:]
        weights[t] = now
        columns = set_of(t)
        predicted = nt_dot(columns, weight)
        residual = (both[:, :width] - predicted * now) * p_row
        score = score + tn_dot(residual.astype(jnp.bfloat16), columns)
    score_ref[...] = score
    first = pl.multiple_of(dom * rows, rows)
    for k in range(2):
        own = weights[2 * tm + k, pl.ds(first, rows), :] * total
        smoothed_ref[k : k + 1, :] = own.T[0:1, :]
    for copy in sends:
        copy.wait_send()


def fused(particles, log_weight, trans_weight, precision):
    steps_here, rows, width = particles.shape
    n_dom = lax.axis_size("dom")
    total = n_dom * rows
    whole = pl.BlockSpec(memory_space=pltpu.VMEM)
    copies = (n_dom // 2 - 1) * 3 + 2 + n_dom // 2
    return pl.pallas_call(
        functools.partial(smoother_kernel, n_dom),
        out_shape=(
            jax.ShapeDtypeStruct((steps_here, rows), jnp.float32),
            jax.ShapeDtypeStruct((width, width), jnp.float32),
        ),
        in_specs=[whole] * 4,
        out_specs=(whole, whole),
        scratch_shapes=[
            pltpu.VMEM((2 * n_dom, 2 * rows + EXTRA, width), jnp.bfloat16),
            pltpu.VMEM((3, total, total), jnp.bfloat16),
            pltpu.VMEM((3, total, width), jnp.float32),
            pltpu.VMEM((4, total, width), jnp.float32),
            pltpu.VMEM((4, total, width), jnp.float32),
            pltpu.VMEM((EXTRA, width), jnp.float32),
            pltpu.SemaphoreType.DMA((copies,)),
            pltpu.SemaphoreType.DMA((2 * n_dom,)),
        ],
        compiler_params=pltpu.CompilerParams(
            collective_id=0, has_side_effects=True, vmem_limit_bytes=48 * 2**20
        ),
    )(particles, log_weight, trans_weight, precision.reshape(1, width))


def plan(particles, log_weight, trans_weight, precision):
    steps_here, rows, width = particles.shape
    n_dom = lax.axis_size("dom")
    total = n_dom * rows
    small = total <= MOST_ROWS and total % (2 * width) == 0 and rows <= width and rows % 16 == 0
    shaped = n_dom % 2 == 0 and lax.axis_size("tm") == 2 and steps_here == 2 and width == 128
    if small and shaped:
        return fused(particles, log_weight, trans_weight, precision)
    return shards(particles, log_weight, trans_weight, precision)


def solution(mesh):
    placed = (P("tm", ("seq", "dom"), None), P("tm", ("seq", "dom")), P(), P())
    return jax.shard_map(
        plan,
        mesh=mesh,
        in_specs=placed,
        out_specs=(P("tm", ("seq", "dom")), P("seq", None)),
        check_vma=False,
    )
```

```python
import functools

import jax
import jax.numpy as jnp
from jax import lax
from jax.experimental import pallas as pl
from jax.experimental.pallas import tpu as pltpu
from jax.sharding import PartitionSpec as P

exact_mode = lax.Precision.HIGHEST


def from_behind(x, axis, by):
    size = lax.axis_size(axis)
    pairs = [(i, i + by) for i in range(size) if 0 <= i + by < size]
    return lax.ppermute(x, axis, pairs)


def block_size(length):
    best = 1
    for trial in range(1, min(length, 512) + 1):
        if length % trial == 0:
            best = trial
    return best


def project_rows(rows, precision, weight_full):
    return jnp.dot(rows.astype(jnp.float32) * precision, weight_full, precision=exact_mode).astype(
        jnp.bfloat16
    )


def pair_scores(row_proj, column_rows, column_bias):
    return (
        jnp.einsum("id,jd->ij", row_proj, column_rows, preferred_element_type=jnp.float32)
        + column_bias[None, :]
    )


def make_norm_fold(row_proj, bias_row, carried, block_in, first_row):
    length = block_in.shape[0]
    size = block_size(length)

    def inner(position, state):
        row_top, row_total = state
        offset = position * size
        column_rows = lax.dynamic_slice_in_dim(block_in, offset, size, 0)
        bias_part = lax.dynamic_slice_in_dim(bias_row, first_row + offset, size, 0)
        scores = pair_scores(row_proj, column_rows, bias_part)
        new_top = jnp.maximum(row_top, jnp.max(scores, axis=1))
        row_total = row_total * jnp.exp(row_top - new_top) + jnp.sum(
            jnp.exp(scores - new_top[:, None]), axis=1
        )
        return (new_top, row_total)

    return lax.fori_loop(0, length // size, inner, carried)


def make_column_fold(row_proj, bias_row, row_norm, row_weight, carried, block_in, first_row):
    length = block_in.shape[0]
    size = block_size(length)

    def inner(position, state):
        moved, column_sums = state
        offset = position * size
        column_rows = lax.dynamic_slice_in_dim(block_in, offset, size, 0)
        bias_part = lax.dynamic_slice_in_dim(bias_row, first_row + offset, size, 0)
        scores = pair_scores(row_proj, column_rows, bias_part)
        backward = (row_weight[:, None] * jnp.exp(scores - row_norm[:, None])).astype(jnp.bfloat16)
        moved = moved + jnp.dot(backward, column_rows, preferred_element_type=jnp.float32)
        column_sums = lax.dynamic_update_slice_in_dim(
            column_sums, jnp.sum(backward.astype(jnp.float32), axis=0), first_row + offset, 0
        )
        return (moved, column_sums)

    return lax.fori_loop(0, length // size, inner, carried)


def shards(particles, log_weight, trans_weight, precision):
    steps_here, rows_here, width = particles.shape
    tm_count = lax.axis_size("tm")
    dom_count = lax.axis_size("dom")
    total_rows = rows_here * dom_count
    tm_place = lax.axis_index("tm")
    is_last = tm_place == tm_count - 1
    weight_full = trans_weight.astype(jnp.float32)
    boundary = from_behind(particles[0], "tm", -1)
    later_sets = [particles[1]] + [boundary]
    later_proj = [project_rows(rows, precision, weight_full) for rows in later_sets]
    biases = []
    for k in range(steps_here):
        predicted = jnp.dot(particles[k], trans_weight.T, preferred_element_type=jnp.float32)
        biases.append(log_weight[k] - 0.5 * jnp.sum(precision * predicted * predicted, axis=1))
    local_bias = jnp.stack(biases)
    full_bias = lax.all_gather(local_bias, "dom", axis=1, tiled=True)
    row_norms = []
    whole = lax.all_gather(particles, "dom", axis=1, tiled=True)
    for k in range(steps_here):
        start_state = (
            jnp.full((rows_here,), -jnp.inf, jnp.float32),
            jnp.zeros((rows_here,), jnp.float32),
        )
        row_top, row_total = make_norm_fold(later_proj[k], full_bias[k], start_state, whole[k], 0)
        row_norms.append(row_top + jnp.log(row_total))
    final_logs = log_weight[steps_here - 1]
    global_top = lax.pmax(jnp.max(final_logs), "dom")
    global_total = lax.psum(jnp.sum(jnp.exp(final_logs - global_top)), "dom")
    final_weights = jnp.exp(final_logs - global_top) / global_total
    carried = (
        jnp.zeros((steps_here, rows_here), jnp.float32),
        jnp.zeros((width, width), jnp.float32),
    )
    for r in range(tm_count):
        if r == 0:
            incoming = jnp.zeros((rows_here,), jnp.float32)
        else:
            incoming = from_behind(carried[0][0], "tm", -1)
        owner = tm_count - 1 - r
        backward_partial_value = jnp.zeros((width, width), jnp.float32)
        outputs = [None] * steps_here
        row_weight = incoming
        for backward_k in range(steps_here - 1, -1, -1):
            column_rows = particles[backward_k]
            backward_start_state = (
                jnp.zeros((rows_here, width), jnp.float32),
                jnp.zeros((total_rows,), jnp.float32),
            )
            moved, column_sums = make_column_fold(
                later_proj[backward_k],
                full_bias[backward_k],
                row_norms[backward_k],
                row_weight,
                backward_start_state,
                whole[backward_k],
                0,
            )
            column_weights = lax.psum_scatter(column_sums, "dom", scatter_dimension=0, tiled=True)
            outer = jnp.dot(
                later_sets[backward_k].astype(jnp.float32).T, moved, precision=exact_mode
            )
            column_float = column_rows.astype(jnp.float32)
            moment = jnp.dot(
                column_float.T * column_weights[None, :], column_float, precision=exact_mode
            )
            backward_partial_value = backward_partial_value + precision[:, None] * (
                outer - jnp.dot(weight_full, moment, precision=exact_mode)
            )
            if backward_k == steps_here - 1:
                column_weights = jnp.where(is_last, final_weights, column_weights)
            outputs[backward_k] = column_weights
            row_weight = column_weights
        is_owner = tm_place == owner
        carried = (
            jnp.where(is_owner, jnp.stack(outputs), carried[0]),
            jnp.where(is_owner, backward_partial_value, carried[1]),
        )
    stacked, partial_value = carried
    score = lax.psum(partial_value, ("dom", "tm"))
    return (stacked * total_rows, score)


MESH = pl.DeviceIdType.MESH
EXTRA = 16
MOST_ROWS = 1024


def nt_dot(a, b):
    return lax.dot_general(a, b, (((1,), (1,)), ((), ())), preferred_element_type=jnp.float32)


def tn_dot(a, b):
    return lax.dot_general(a, b, (((0,), (0,)), ((), ())), preferred_element_type=jnp.float32)


def nn_dot(a, b):
    return jnp.dot(a, b, preferred_element_type=jnp.float32)


def split_three(x):
    high = x.astype(jnp.bfloat16)
    rest = x - high.astype(jnp.float32)
    middle = rest.astype(jnp.bfloat16)
    low = (rest - middle.astype(jnp.float32)).astype(jnp.bfloat16)
    return high, middle, low


def smoother_kernel(
    n_dom, x_hbm, lw_hbm, w_hbm, p_hbm, smoothed_ref, score_ref,
    lw_ref, w_ref, p_ref, held, kernel_rows, stats, inverse_norm, bias, weights, stage, in_sem, send_sem, recv_sem,
):
    rows, width = x_hbm.shape[1:]
    total = n_dom * rows
    steps = 4
    half = total // 2
    dom = lax.axis_index("dom")
    tm = lax.axis_index("tm")
    group, side = dom // 2, dom % 2
    high, low = group // 2, group % 2
    near = 2 * high + 1 - low
    mirror = 2 * (1 - high) + low
    opposite = 2 * (1 - high) + 1 - low
    across = dom + 1 - 2 * side
    other = 1 - tm
    mine = tm * n_dom + group
    peers = [2 * g + side for g in (near, mirror, opposite)]

    loads = [
        pltpu.make_async_copy(source, target, in_sem.at[i])
        for i, (source, target) in enumerate(
            [
                (w_hbm, w_ref),
                (p_hbm, p_ref),
                (lw_hbm, lw_ref),
                (x_hbm.at[0], held.at[mine, 0:rows]),
                (x_hbm.at[1], held.at[mine, rows : 2 * rows]),
            ]
        )
    ]
    for load in loads:
        load.start()

    barrier = pltpu.get_barrier_semaphore()
    targets = [(peer, tm) for peer in peers] + [(across, tm), (dom, other)]
    for to_dom, to_tm in targets:
        pl.semaphore_signal(
            barrier, inc=1, device_id={"dom": to_dom, "tm": to_tm}, device_id_type=MESH
        )

    for load in loads:
        load.wait()
    weight = w_ref[...]
    p_row = p_ref[...]
    p_down = jnp.broadcast_to(p_row, (width, width)).T
    stage[...] = jnp.zeros_like(stage)
    terms = []
    for k in range(2):
        x_k = held[mine, k * rows : (k + 1) * rows, :]
        predicted = nt_dot(weight, x_k)
        energy = jnp.sum(p_down[:, :rows] * predicted * predicted, axis=0, keepdims=True)
        terms.append(lw_ref[k : k + 1, :] - 0.5 * energy)
    terms.append(lw_ref[1:2, :])
    for q in range(3):
        for piece, value in enumerate(split_three(terms[q])):
            row = 3 * piece + q
            stage[row : row + 1, 0:rows] = value.astype(jnp.float32)
    held[mine, 2 * rows : 2 * rows + EXTRA, :] = stage[...].astype(jnp.bfloat16)

    pl.semaphore_wait(barrier, len(targets))

    sends = []

    def transfer(source, target, index, to_dom, to_tm):
        return pltpu.make_async_remote_copy(
            src_ref=held.at[source],
            dst_ref=held.at[target],
            send_sem=send_sem.at[index],
            recv_sem=recv_sem.at[target],
            device_id={"dom": to_dom, "tm": to_tm},
            device_id_type=MESH,
        )

    def send(source, target, to_dom, to_tm):
        copy = transfer(source, target, len(sends), to_dom, to_tm)
        copy.start()
        sends.append(copy)

    def arrive(slot):
        transfer(slot, slot, 0, dom, other).wait_recv()

    base, far_base = tm * n_dom, other * n_dom
    part = n_dom // 2
    for peer in peers:
        send(mine, mine, peer, tm)
    send(mine, mine + part, across, tm)
    send(mine, mine, dom, other)

    scaled = jnp.concatenate(split_three(p_down * weight.astype(jnp.float32)), axis=1)
    line = lax.broadcasted_iota(jnp.int32, (EXTRA, 3 * width), 0)
    which = lax.broadcasted_iota(jnp.int32, (EXTRA, 3 * width), 1) // width
    pick = jnp.where((line < 9) & (line % 3 == which), 1.0, 0.0).astype(jnp.bfloat16)

    def set_of(at, k):
        return held[pl.ds(at, part), k * rows : (k + 1) * rows, :].reshape(half, width)

    def spread_bias(h):
        for c in range(2):
            for g in range(part):
                s = c * n_dom + h * part + g
                spread = tn_dot(held[s, 2 * rows : 2 * rows + EXTRA, :], pick)
                for k in range(2):
                    t = 2 * c + k
                    q = 2 if t == steps - 1 else k
                    bias[t, h, g * rows : (g + 1) * rows, :] = spread[:rows, q * width : (q + 1) * width]

    def tile(t, column_at, column_k, row_at, row_k, j, i):
        wide = nn_dot(set_of(row_at + i * part, row_k), scaled)
        projected = (
            wide[:, :width] + (wide[:, width : 2 * width] + wide[:, 2 * width :])
        ).astype(jnp.bfloat16)
        scores = nt_dot(set_of(column_at + j * part, column_k), projected)
        scores = scores + jnp.concatenate([bias[t, j]] * (half // width), axis=1)
        top = jnp.max(scores, axis=0, keepdims=True)
        terms = jnp.exp(scores - top)
        kernel_rows[t, j, :, i * half : (i + 1) * half] = terms.astype(jnp.bfloat16)
        stats[t, 2 * j + i, 0:1, :] = top
        stats[t, 2 * j + i, 1:2, :] = jnp.sum(terms, axis=0, keepdims=True)

    own_t = (2 * tm, base, 0, base, 1)
    middle_t = (1, 0, 1, n_dom, 0)
    other_t = (2 * other, far_base, 0, far_base, 1)

    for n, g in enumerate((near, mirror, opposite)):
        arrive(base + g)
        send(base + g, base + g + part, across, tm)
        send(base + g, base + g, dom, other)
        if n == 0:
            arrive(base + part + group)
            send(base + part + group, base + part + group, dom, other)
    for g in range(part):
        arrive(far_base + g)
    spread_bias(0)
    for case in (own_t, middle_t, other_t):
        tile(*case, 0, 0)
    for g in (near, mirror, opposite):
        arrive(base + part + g)
        send(base + part + g, base + part + g, dom, other)
    for g in range(part):
        arrive(far_base + part + g)
    spread_bias(1)

    last = bias[steps - 1].reshape(total, width)
    last = jnp.exp(last - jnp.max(last, axis=0, keepdims=True))
    weights[steps - 1] = last / jnp.sum(last, axis=0, keepdims=True)

    for case in (own_t, middle_t, other_t):
        for j, i in ((0, 1), (1, 0), (1, 1)):
            tile(*case, j, i)

    score = jnp.zeros((width, width), jnp.float32)
    for t in range(steps - 2, -1, -1):
        for i in range(2):
            tops = [stats[t, 2 * j + i, 0:1, :] for j in range(2)]
            top = jnp.maximum(tops[0], tops[1])
            scales = [jnp.exp(tops[j] - top) for j in range(2)]
            norm = sum(scales[j] * stats[t, 2 * j + i, 1:2, :] for j in range(2))
            for j in range(2):
                inverse = scales[j] / norm
                for b in range(half // width):
                    at = i * half + b * width
                    inverse_norm[t, j, at : at + width, :] = jnp.broadcast_to(
                        inverse[:, b * width : (b + 1) * width], (width, width)
                    ).T
    for t in range(steps - 2, -1, -1):
        at, k = (t // 2) * n_dom, t % 2
        later_at, later_k = ((t + 1) // 2) * n_dom, (t + 1) % 2
        later = jnp.concatenate([set_of(later_at + i * part, later_k) for i in range(2)], axis=0)
        later = later.astype(jnp.float32)
        for j in range(2):
            ratio = weights[t + 1] * inverse_norm[t, j]
            right = jnp.concatenate(
                [(ratio * later).astype(jnp.bfloat16), ratio.astype(jnp.bfloat16)], axis=1
            )
            both = nn_dot(kernel_rows[t, j], right)
            now = both[:, width:]
            weights[t, j * half : (j + 1) * half, :] = now
            columns = set_of(at + j * part, k)
            predicted = nt_dot(columns, weight)
            residual = (both[:, :width] - predicted * now).astype(jnp.bfloat16)
            score = score + tn_dot(residual, columns)
    score_ref[...] = score
    first = pl.multiple_of(group * rows, rows)
    for k in range(2):
        own = weights[2 * tm + k, pl.ds(first, rows), :]
        smoothed_ref[k : k + 1, :] = own.T[0:1, :]
    for copy in sends:
        copy.wait_send()


def fused(particles, log_weight, trans_weight, precision):
    steps_here, rows, width = particles.shape
    n_dom = lax.axis_size("dom")
    total = n_dom * rows
    whole = pl.BlockSpec(memory_space=pltpu.VMEM)
    copies = (n_dom // 2 - 1) * 3 + 2 + n_dom // 2
    smoothed, score = pl.pallas_call(
        functools.partial(smoother_kernel, n_dom),
        out_shape=(
            jax.ShapeDtypeStruct((steps_here, rows), jnp.float32),
            jax.ShapeDtypeStruct((width, width), jnp.float32),
        ),
        in_specs=[pl.BlockSpec(memory_space=pltpu.HBM)] * 4,
        out_specs=(whole, whole),
        scratch_shapes=[
            pltpu.VMEM((steps_here, rows), jnp.float32),
            pltpu.VMEM((width, width), jnp.bfloat16),
            pltpu.VMEM((1, width), jnp.float32),
            pltpu.VMEM((2 * n_dom, 2 * rows + EXTRA, width), jnp.bfloat16),
            pltpu.VMEM((3, 2, total // 2, total), jnp.bfloat16),
            pltpu.VMEM((3, 4, 8, total // 2), jnp.float32),
            pltpu.VMEM((3, 2, total, width), jnp.float32),
            pltpu.VMEM((4, 2, total // 2, width), jnp.float32),
            pltpu.VMEM((4, total, width), jnp.float32),
            pltpu.VMEM((EXTRA, width), jnp.float32),
            pltpu.SemaphoreType.DMA((5,)),
            pltpu.SemaphoreType.DMA((copies,)),
            pltpu.SemaphoreType.DMA((2 * n_dom,)),
        ],
        compiler_params=pltpu.CompilerParams(
            collective_id=0, has_side_effects=True, vmem_limit_bytes=64 * 2**20
        ),
    )(particles, log_weight, trans_weight, precision.reshape(1, width))
    return smoothed * total, score * precision[:, None]


def plan(particles, log_weight, trans_weight, precision):
    steps_here, rows, width = particles.shape
    n_dom = lax.axis_size("dom")
    total = n_dom * rows
    small = total <= MOST_ROWS and total % (2 * width) == 0 and rows <= width and rows % 16 == 0
    shaped = n_dom == 8 and lax.axis_size("tm") == 2 and steps_here == 2 and width == 128
    if small and shaped:
        return fused(particles, log_weight, trans_weight, precision)
    return shards(particles, log_weight, trans_weight, precision)


def solution(mesh):
    placed = (P("tm", ("seq", "dom"), None), P("tm", ("seq", "dom")), P(), P())
    return jax.shard_map(
        plan,
        mesh=mesh,
        in_specs=placed,
        out_specs=(P("tm", ("seq", "dom")), P("seq", None)),
        check_vma=False,
    )
```

```python
import functools

import jax
import jax.numpy as jnp
from jax import lax
from jax.experimental import pallas as pl
from jax.experimental.pallas import tpu as pltpu
from jax.sharding import PartitionSpec as P

exact_mode = lax.Precision.HIGHEST


def from_behind(x, axis, by):
    size = lax.axis_size(axis)
    pairs = [(i, i + by) for i in range(size) if 0 <= i + by < size]
    return lax.ppermute(x, axis, pairs)


def block_size(length):
    best = 1
    for trial in range(1, min(length, 512) + 1):
        if length % trial == 0:
            best = trial
    return best


def project_rows(rows, precision, weight_full):
    return jnp.dot(rows.astype(jnp.float32) * precision, weight_full, precision=exact_mode).astype(
        jnp.bfloat16
    )


def pair_scores(row_proj, column_rows, column_bias):
    return (
        jnp.einsum("id,jd->ij", row_proj, column_rows, preferred_element_type=jnp.float32)
        + column_bias[None, :]
    )


def make_norm_fold(row_proj, bias_row, carried, block_in, first_row):
    length = block_in.shape[0]
    size = block_size(length)

    def inner(position, state):
        row_top, row_total = state
        offset = position * size
        column_rows = lax.dynamic_slice_in_dim(block_in, offset, size, 0)
        bias_part = lax.dynamic_slice_in_dim(bias_row, first_row + offset, size, 0)
        scores = pair_scores(row_proj, column_rows, bias_part)
        new_top = jnp.maximum(row_top, jnp.max(scores, axis=1))
        row_total = row_total * jnp.exp(row_top - new_top) + jnp.sum(
            jnp.exp(scores - new_top[:, None]), axis=1
        )
        return (new_top, row_total)

    return lax.fori_loop(0, length // size, inner, carried)


def make_column_fold(row_proj, bias_row, row_norm, row_weight, carried, block_in, first_row):
    length = block_in.shape[0]
    size = block_size(length)

    def inner(position, state):
        moved, column_sums = state
        offset = position * size
        column_rows = lax.dynamic_slice_in_dim(block_in, offset, size, 0)
        bias_part = lax.dynamic_slice_in_dim(bias_row, first_row + offset, size, 0)
        scores = pair_scores(row_proj, column_rows, bias_part)
        backward = (row_weight[:, None] * jnp.exp(scores - row_norm[:, None])).astype(jnp.bfloat16)
        moved = moved + jnp.dot(backward, column_rows, preferred_element_type=jnp.float32)
        column_sums = lax.dynamic_update_slice_in_dim(
            column_sums, jnp.sum(backward.astype(jnp.float32), axis=0), first_row + offset, 0
        )
        return (moved, column_sums)

    return lax.fori_loop(0, length // size, inner, carried)


def shards(particles, log_weight, trans_weight, precision):
    steps_here, rows_here, width = particles.shape
    tm_count = lax.axis_size("tm")
    dom_count = lax.axis_size("dom")
    total_rows = rows_here * dom_count
    tm_place = lax.axis_index("tm")
    is_last = tm_place == tm_count - 1
    weight_full = trans_weight.astype(jnp.float32)
    boundary = from_behind(particles[0], "tm", -1)
    later_sets = [particles[1]] + [boundary]
    later_proj = [project_rows(rows, precision, weight_full) for rows in later_sets]
    biases = []
    for k in range(steps_here):
        predicted = jnp.dot(particles[k], trans_weight.T, preferred_element_type=jnp.float32)
        biases.append(log_weight[k] - 0.5 * jnp.sum(precision * predicted * predicted, axis=1))
    local_bias = jnp.stack(biases)
    full_bias = lax.all_gather(local_bias, "dom", axis=1, tiled=True)
    row_norms = []
    whole = lax.all_gather(particles, "dom", axis=1, tiled=True)
    for k in range(steps_here):
        start_state = (
            jnp.full((rows_here,), -jnp.inf, jnp.float32),
            jnp.zeros((rows_here,), jnp.float32),
        )
        row_top, row_total = make_norm_fold(later_proj[k], full_bias[k], start_state, whole[k], 0)
        row_norms.append(row_top + jnp.log(row_total))
    final_logs = log_weight[steps_here - 1]
    global_top = lax.pmax(jnp.max(final_logs), "dom")
    global_total = lax.psum(jnp.sum(jnp.exp(final_logs - global_top)), "dom")
    final_weights = jnp.exp(final_logs - global_top) / global_total
    carried = (
        jnp.zeros((steps_here, rows_here), jnp.float32),
        jnp.zeros((width, width), jnp.float32),
    )
    for r in range(tm_count):
        if r == 0:
            incoming = jnp.zeros((rows_here,), jnp.float32)
        else:
            incoming = from_behind(carried[0][0], "tm", -1)
        owner = tm_count - 1 - r
        backward_partial_value = jnp.zeros((width, width), jnp.float32)
        outputs = [None] * steps_here
        row_weight = incoming
        for backward_k in range(steps_here - 1, -1, -1):
            column_rows = particles[backward_k]
            backward_start_state = (
                jnp.zeros((rows_here, width), jnp.float32),
                jnp.zeros((total_rows,), jnp.float32),
            )
            moved, column_sums = make_column_fold(
                later_proj[backward_k],
                full_bias[backward_k],
                row_norms[backward_k],
                row_weight,
                backward_start_state,
                whole[backward_k],
                0,
            )
            column_weights = lax.psum_scatter(column_sums, "dom", scatter_dimension=0, tiled=True)
            outer = jnp.dot(
                later_sets[backward_k].astype(jnp.float32).T, moved, precision=exact_mode
            )
            column_float = column_rows.astype(jnp.float32)
            moment = jnp.dot(
                column_float.T * column_weights[None, :], column_float, precision=exact_mode
            )
            backward_partial_value = backward_partial_value + precision[:, None] * (
                outer - jnp.dot(weight_full, moment, precision=exact_mode)
            )
            if backward_k == steps_here - 1:
                column_weights = jnp.where(is_last, final_weights, column_weights)
            outputs[backward_k] = column_weights
            row_weight = column_weights
        is_owner = tm_place == owner
        carried = (
            jnp.where(is_owner, jnp.stack(outputs), carried[0]),
            jnp.where(is_owner, backward_partial_value, carried[1]),
        )
    stacked, partial_value = carried
    score = lax.psum(partial_value, ("dom", "tm"))
    return (stacked * total_rows, score)


MESH = pl.DeviceIdType.MESH
EXTRA = 16
MOST_ROWS = 1024


def nt_dot(a, b):
    return lax.dot_general(a, b, (((1,), (1,)), ((), ())), preferred_element_type=jnp.float32)


def tn_dot(a, b):
    return lax.dot_general(a, b, (((0,), (0,)), ((), ())), preferred_element_type=jnp.float32)


def nn_dot(a, b):
    return jnp.dot(a, b, preferred_element_type=jnp.float32)


def split_three(x):
    high = x.astype(jnp.bfloat16)
    rest = x - high.astype(jnp.float32)
    middle = rest.astype(jnp.bfloat16)
    low = (rest - middle.astype(jnp.float32)).astype(jnp.bfloat16)
    return high, middle, low


def smoother_kernel(
    n_dom, x_hbm, lw_hbm, w_hbm, p_hbm, smoothed_ref, score_ref,
    lw_ref, w_ref, p_ref, held, kernel_rows, stats, inverse_norm, bias, weights, stage, in_sem, send_sem, recv_sem,
):
    rows, width = x_hbm.shape[1:]
    total = n_dom * rows
    steps = 4
    half = total // 2
    dom = lax.axis_index("dom")
    tm = lax.axis_index("tm")
    group, side = dom // 2, dom % 2
    high, low = group // 2, group % 2
    near = 2 * high + 1 - low
    mirror = 2 * (1 - high) + low
    opposite = 2 * (1 - high) + 1 - low
    across = dom + 1 - 2 * side
    other = 1 - tm
    mine = tm * n_dom + group
    peers = [2 * g + side for g in (near, mirror, opposite)]

    loads = [
        pltpu.make_async_copy(source, target, in_sem.at[i])
        for i, (source, target) in enumerate(
            [
                (w_hbm, w_ref),
                (p_hbm, p_ref),
                (lw_hbm, lw_ref),
                (x_hbm.at[0], held.at[mine, 0:rows]),
                (x_hbm.at[1], held.at[mine, rows : 2 * rows]),
            ]
        )
    ]
    for load in loads:
        load.start()

    barrier = pltpu.get_barrier_semaphore()
    targets = [(peer, tm) for peer in peers] + [(across, tm), (dom, other)]
    for to_dom, to_tm in targets:
        pl.semaphore_signal(
            barrier, inc=1, device_id={"dom": to_dom, "tm": to_tm}, device_id_type=MESH
        )

    for load in loads:
        load.wait()
    weight = w_ref[...]
    p_row = p_ref[...]
    p_down = jnp.broadcast_to(p_row, (width, width)).T
    stage[...] = jnp.zeros_like(stage)
    terms = []
    for k in range(2):
        x_k = held[mine, k * rows : (k + 1) * rows, :]
        predicted = nt_dot(weight, x_k)
        energy = jnp.sum(p_down[:, :rows] * predicted * predicted, axis=0, keepdims=True)
        terms.append(lw_ref[k : k + 1, :] - 0.5 * energy)
    terms.append(lw_ref[1:2, :])
    for q in range(3):
        for piece, value in enumerate(split_three(terms[q])):
            row = 3 * piece + q
            stage[row : row + 1, 0:rows] = value.astype(jnp.float32)
    held[mine, 2 * rows : 2 * rows + EXTRA, :] = stage[...].astype(jnp.bfloat16)

    pl.semaphore_wait(barrier, len(targets))

    sends = []

    def transfer(source, target, index, to_dom, to_tm):
        return pltpu.make_async_remote_copy(
            src_ref=held.at[source],
            dst_ref=held.at[target],
            send_sem=send_sem.at[index],
            recv_sem=recv_sem.at[target],
            device_id={"dom": to_dom, "tm": to_tm},
            device_id_type=MESH,
        )

    def send(source, target, to_dom, to_tm):
        copy = transfer(source, target, len(sends), to_dom, to_tm)
        copy.start()
        sends.append(copy)

    def arrive(slot):
        transfer(slot, slot, 0, dom, other).wait_recv()

    base, far_base = tm * n_dom, other * n_dom
    part = n_dom // 2
    for peer in peers:
        send(mine, mine, peer, tm)
    send(mine, mine + part, across, tm)
    send(mine, mine, dom, other)

    scaled = jnp.concatenate(split_three(p_down * weight.astype(jnp.float32)), axis=1)
    line = lax.broadcasted_iota(jnp.int32, (EXTRA, 3 * width), 0)
    which = lax.broadcasted_iota(jnp.int32, (EXTRA, 3 * width), 1) // width
    pick = jnp.where((line < 9) & (line % 3 == which), 1.0, 0.0).astype(jnp.bfloat16)

    def set_of(at, k):
        return held[pl.ds(at, part), k * rows : (k + 1) * rows, :].reshape(half, width)

    def spread_bias(h):
        for c in range(2):
            for g in range(part):
                s = c * n_dom + h * part + g
                spread = tn_dot(held[s, 2 * rows : 2 * rows + EXTRA, :], pick)
                for k in range(2):
                    t = 2 * c + k
                    q = 2 if t == steps - 1 else k
                    bias[t, h, g * rows : (g + 1) * rows, :] = spread[:rows, q * width : (q + 1) * width]

    def tile(t, column_at, column_k, row_at, row_k, j, i):
        wide = nn_dot(set_of(row_at + i * part, row_k), scaled)
        projected = (
            wide[:, :width] + (wide[:, width : 2 * width] + wide[:, 2 * width :])
        ).astype(jnp.bfloat16)
        scores = nt_dot(set_of(column_at + j * part, column_k), projected)
        scores = scores + jnp.concatenate([bias[t, j]] * (half // width), axis=1)
        top = jnp.max(scores, axis=0, keepdims=True)
        terms = jnp.exp(scores - top)
        kernel_rows[t, j, :, i * half : (i + 1) * half] = terms.astype(jnp.bfloat16)
        stats[t, 2 * j + i, 0:1, :] = top
        stats[t, 2 * j + i, 1:2, :] = jnp.sum(terms, axis=0, keepdims=True)

    def tall_tile(t, column_at, column_k, row_at, row_k):
        wide = nn_dot(set_of(row_at + part, row_k), scaled)
        projected = (
            wide[:, :width] + (wide[:, width : 2 * width] + wide[:, 2 * width :])
        ).astype(jnp.bfloat16)
        columns = [set_of(column_at + j * part, column_k) for j in range(2)]
        scores = nt_dot(jnp.concatenate(columns, axis=0), projected)
        column_bias = bias[t].reshape(total, width)
        scores = scores + jnp.concatenate([column_bias] * (half // width), axis=1)
        top = jnp.max(scores, axis=0, keepdims=True)
        terms = jnp.exp(scores - top)
        rounded = terms.astype(jnp.bfloat16)
        sums = (jnp.sum(terms, axis=0, keepdims=True), jnp.zeros_like(top))
        for j in range(2):
            kernel_rows[t, j, :, half:] = rounded[j * half : (j + 1) * half]
            stats[t, 2 * j + 1, 0:1, :] = top
            stats[t, 2 * j + 1, 1:2, :] = sums[j]

    own_t = (2 * tm, base, 0, base, 1)
    middle_t = (1, 0, 1, n_dom, 0)
    other_t = (2 * other, far_base, 0, far_base, 1)

    for n, g in enumerate((near, mirror, opposite)):
        arrive(base + g)
        send(base + g, base + g + part, across, tm)
        send(base + g, base + g, dom, other)
        if n == 0:
            arrive(base + part + group)
            send(base + part + group, base + part + group, dom, other)
    for g in range(part):
        arrive(far_base + g)
    spread_bias(0)
    for case in (own_t, middle_t, other_t):
        tile(*case, 0, 0)
    for g in (near, mirror, opposite):
        arrive(base + part + g)
        send(base + part + g, base + part + g, dom, other)
    for g in range(part):
        arrive(far_base + part + g)
    spread_bias(1)

    last = bias[steps - 1].reshape(total, width)
    last = jnp.exp(last - jnp.max(last, axis=0, keepdims=True))
    weights[steps - 1] = last / jnp.sum(last, axis=0, keepdims=True)

    for case in (own_t, middle_t, other_t):
        tile(*case, 1, 0)
        tall_tile(*case)

    score = jnp.zeros((width, width), jnp.float32)
    for t in range(steps - 2, -1, -1):
        for i in range(2):
            tops = [stats[t, 2 * j + i, 0:1, :] for j in range(2)]
            top = jnp.maximum(tops[0], tops[1])
            scales = [jnp.exp(tops[j] - top) for j in range(2)]
            norm = sum(scales[j] * stats[t, 2 * j + i, 1:2, :] for j in range(2))
            for j in range(2):
                inverse = scales[j] / norm
                for b in range(half // width):
                    at = i * half + b * width
                    inverse_norm[t, j, at : at + width, :] = jnp.broadcast_to(
                        inverse[:, b * width : (b + 1) * width], (width, width)
                    ).T
    for t in range(steps - 2, -1, -1):
        at, k = (t // 2) * n_dom, t % 2
        later_at, later_k = ((t + 1) // 2) * n_dom, (t + 1) % 2
        later = jnp.concatenate([set_of(later_at + i * part, later_k) for i in range(2)], axis=0)
        later = later.astype(jnp.float32)
        for j in range(2):
            ratio = weights[t + 1] * inverse_norm[t, j]
            right = jnp.concatenate(
                [(ratio * later).astype(jnp.bfloat16), ratio.astype(jnp.bfloat16)], axis=1
            )
            both = nn_dot(kernel_rows[t, j], right)
            now = both[:, width:]
            weights[t, j * half : (j + 1) * half, :] = now
            columns = set_of(at + j * part, k)
            predicted = nt_dot(columns, weight)
            residual = (both[:, :width] - predicted * now).astype(jnp.bfloat16)
            score = score + tn_dot(residual, columns)
    score_ref[...] = score * p_down
    first = pl.multiple_of(group * rows, rows)
    for k in range(2):
        own = weights[2 * tm + k, pl.ds(first, rows), :]
        smoothed_ref[k : k + 1, :] = own.T[0:1, :] * total
    for copy in sends:
        copy.wait_send()


def hand_over(a_in, b_in, a_out, b_out, a_held, b_held, sems):
    arriving = [
        pltpu.make_async_copy(a_in, a_held, sems.at[0]),
        pltpu.make_async_copy(b_in, b_held, sems.at[1]),
    ]
    leaving = [
        pltpu.make_async_copy(a_held, a_out, sems.at[2]),
        pltpu.make_async_copy(b_held, b_out, sems.at[3]),
    ]
    for copy in arriving:
        copy.start()
    for first, then in zip(arriving, leaving):
        first.wait()
        then.start()
    for copy in leaving:
        copy.wait()


def fused(particles, log_weight, trans_weight, precision):
    steps_here, rows, width = particles.shape
    n_dom = lax.axis_size("dom")
    total = n_dom * rows
    whole = pl.BlockSpec(memory_space=pltpu.VMEM)
    copies = (n_dom // 2 - 1) * 3 + 2 + n_dom // 2
    smoothed, score = pl.pallas_call(
        functools.partial(smoother_kernel, n_dom),
        out_shape=(
            jax.ShapeDtypeStruct((steps_here, rows), jnp.float32),
            jax.ShapeDtypeStruct((width, width), jnp.float32),
        ),
        in_specs=[pl.BlockSpec(memory_space=pltpu.HBM)] * 4,
        out_specs=(whole, whole),
        scratch_shapes=[
            pltpu.VMEM((steps_here, rows), jnp.float32),
            pltpu.VMEM((width, width), jnp.bfloat16),
            pltpu.VMEM((1, width), jnp.float32),
            pltpu.VMEM((2 * n_dom, 2 * rows + EXTRA, width), jnp.bfloat16),
            pltpu.VMEM((3, 2, total // 2, total), jnp.bfloat16),
            pltpu.VMEM((3, 4, 8, total // 2), jnp.float32),
            pltpu.VMEM((3, 2, total, width), jnp.float32),
            pltpu.VMEM((4, 2, total // 2, width), jnp.float32),
            pltpu.VMEM((4, total, width), jnp.float32),
            pltpu.VMEM((EXTRA, width), jnp.float32),
            pltpu.SemaphoreType.DMA((5,)),
            pltpu.SemaphoreType.DMA((copies,)),
            pltpu.SemaphoreType.DMA((2 * n_dom,)),
        ],
        compiler_params=pltpu.CompilerParams(
            collective_id=0, has_side_effects=True, vmem_limit_bytes=64 * 2**20
        ),
    )(particles, log_weight, trans_weight, precision.reshape(1, width))
    return pl.pallas_call(
        hand_over,
        out_shape=(
            jax.ShapeDtypeStruct((steps_here, rows), jnp.float32),
            jax.ShapeDtypeStruct((width, width), jnp.float32),
        ),
        in_specs=[pl.BlockSpec(memory_space=pltpu.HBM)] * 2,
        out_specs=(pl.BlockSpec(memory_space=pltpu.HBM),) * 2,
        scratch_shapes=[
            pltpu.VMEM((steps_here, rows), jnp.float32),
            pltpu.VMEM((width, width), jnp.float32),
            pltpu.SemaphoreType.DMA((4,)),
        ],
        compiler_params=pltpu.CompilerParams(vmem_limit_bytes=64 * 2**20),
    )(smoothed, score)


def plan(particles, log_weight, trans_weight, precision):
    steps_here, rows, width = particles.shape
    n_dom = lax.axis_size("dom")
    total = n_dom * rows
    small = total <= MOST_ROWS and total % (2 * width) == 0 and rows <= width and rows % 16 == 0
    shaped = n_dom == 8 and lax.axis_size("tm") == 2 and steps_here == 2 and width == 128
    if small and shaped:
        return fused(particles, log_weight, trans_weight, precision)
    return shards(particles, log_weight, trans_weight, precision)


def solution(mesh):
    placed = (P("tm", ("seq", "dom"), None), P("tm", ("seq", "dom")), P(), P())
    return jax.shard_map(
        plan,
        mesh=mesh,
        in_specs=placed,
        out_specs=(P("tm", ("seq", "dom")), P("seq", None)),
        check_vma=False,
    )
```

```python
import functools

import jax
import jax.numpy as jnp
from jax import lax
from jax.experimental import pallas as pl
from jax.experimental.pallas import tpu as pltpu
from jax.sharding import PartitionSpec as P

exact_mode = lax.Precision.HIGHEST


def from_behind(x, axis, by):
    size = lax.axis_size(axis)
    pairs = [(i, i + by) for i in range(size) if 0 <= i + by < size]
    return lax.ppermute(x, axis, pairs)


def block_size(length):
    best = 1
    for trial in range(1, min(length, 512) + 1):
        if length % trial == 0:
            best = trial
    return best


def project_rows(rows, precision, weight_full):
    return jnp.dot(rows.astype(jnp.float32) * precision, weight_full, precision=exact_mode).astype(
        jnp.bfloat16
    )


def pair_scores(row_proj, column_rows, column_bias):
    return (
        jnp.einsum("id,jd->ij", row_proj, column_rows, preferred_element_type=jnp.float32)
        + column_bias[None, :]
    )


def make_norm_fold(row_proj, bias_row, carried, block_in, first_row):
    length = block_in.shape[0]
    size = block_size(length)

    def inner(position, state):
        row_top, row_total = state
        offset = position * size
        column_rows = lax.dynamic_slice_in_dim(block_in, offset, size, 0)
        bias_part = lax.dynamic_slice_in_dim(bias_row, first_row + offset, size, 0)
        scores = pair_scores(row_proj, column_rows, bias_part)
        new_top = jnp.maximum(row_top, jnp.max(scores, axis=1))
        row_total = row_total * jnp.exp(row_top - new_top) + jnp.sum(
            jnp.exp(scores - new_top[:, None]), axis=1
        )
        return (new_top, row_total)

    return lax.fori_loop(0, length // size, inner, carried)


def make_column_fold(row_proj, bias_row, row_norm, row_weight, carried, block_in, first_row):
    length = block_in.shape[0]
    size = block_size(length)

    def inner(position, state):
        moved, column_sums = state
        offset = position * size
        column_rows = lax.dynamic_slice_in_dim(block_in, offset, size, 0)
        bias_part = lax.dynamic_slice_in_dim(bias_row, first_row + offset, size, 0)
        scores = pair_scores(row_proj, column_rows, bias_part)
        backward = (row_weight[:, None] * jnp.exp(scores - row_norm[:, None])).astype(jnp.bfloat16)
        moved = moved + jnp.dot(backward, column_rows, preferred_element_type=jnp.float32)
        column_sums = lax.dynamic_update_slice_in_dim(
            column_sums, jnp.sum(backward.astype(jnp.float32), axis=0), first_row + offset, 0
        )
        return (moved, column_sums)

    return lax.fori_loop(0, length // size, inner, carried)


def shards(particles, log_weight, trans_weight, precision):
    steps_here, rows_here, width = particles.shape
    tm_count = lax.axis_size("tm")
    dom_count = lax.axis_size("dom")
    total_rows = rows_here * dom_count
    tm_place = lax.axis_index("tm")
    is_last = tm_place == tm_count - 1
    weight_full = trans_weight.astype(jnp.float32)
    boundary = from_behind(particles[0], "tm", -1)
    later_sets = [particles[1]] + [boundary]
    later_proj = [project_rows(rows, precision, weight_full) for rows in later_sets]
    biases = []
    for k in range(steps_here):
        predicted = jnp.dot(particles[k], trans_weight.T, preferred_element_type=jnp.float32)
        biases.append(log_weight[k] - 0.5 * jnp.sum(precision * predicted * predicted, axis=1))
    local_bias = jnp.stack(biases)
    full_bias = lax.all_gather(local_bias, "dom", axis=1, tiled=True)
    row_norms = []
    whole = lax.all_gather(particles, "dom", axis=1, tiled=True)
    for k in range(steps_here):
        start_state = (
            jnp.full((rows_here,), -jnp.inf, jnp.float32),
            jnp.zeros((rows_here,), jnp.float32),
        )
        row_top, row_total = make_norm_fold(later_proj[k], full_bias[k], start_state, whole[k], 0)
        row_norms.append(row_top + jnp.log(row_total))
    final_logs = log_weight[steps_here - 1]
    global_top = lax.pmax(jnp.max(final_logs), "dom")
    global_total = lax.psum(jnp.sum(jnp.exp(final_logs - global_top)), "dom")
    final_weights = jnp.exp(final_logs - global_top) / global_total
    carried = (
        jnp.zeros((steps_here, rows_here), jnp.float32),
        jnp.zeros((width, width), jnp.float32),
    )
    for r in range(tm_count):
        if r == 0:
            incoming = jnp.zeros((rows_here,), jnp.float32)
        else:
            incoming = from_behind(carried[0][0], "tm", -1)
        owner = tm_count - 1 - r
        backward_partial_value = jnp.zeros((width, width), jnp.float32)
        outputs = [None] * steps_here
        row_weight = incoming
        for backward_k in range(steps_here - 1, -1, -1):
            column_rows = particles[backward_k]
            backward_start_state = (
                jnp.zeros((rows_here, width), jnp.float32),
                jnp.zeros((total_rows,), jnp.float32),
            )
            moved, column_sums = make_column_fold(
                later_proj[backward_k],
                full_bias[backward_k],
                row_norms[backward_k],
                row_weight,
                backward_start_state,
                whole[backward_k],
                0,
            )
            column_weights = lax.psum_scatter(column_sums, "dom", scatter_dimension=0, tiled=True)
            outer = jnp.dot(
                later_sets[backward_k].astype(jnp.float32).T, moved, precision=exact_mode
            )
            column_float = column_rows.astype(jnp.float32)
            moment = jnp.dot(
                column_float.T * column_weights[None, :], column_float, precision=exact_mode
            )
            backward_partial_value = backward_partial_value + precision[:, None] * (
                outer - jnp.dot(weight_full, moment, precision=exact_mode)
            )
            if backward_k == steps_here - 1:
                column_weights = jnp.where(is_last, final_weights, column_weights)
            outputs[backward_k] = column_weights
            row_weight = column_weights
        is_owner = tm_place == owner
        carried = (
            jnp.where(is_owner, jnp.stack(outputs), carried[0]),
            jnp.where(is_owner, backward_partial_value, carried[1]),
        )
    stacked, partial_value = carried
    score = lax.psum(partial_value, ("dom", "tm"))
    return (stacked * total_rows, score)


MESH = pl.DeviceIdType.MESH
EXTRA = 16
MOST_ROWS = 1024


def nt_dot(a, b):
    return lax.dot_general(a, b, (((1,), (1,)), ((), ())), preferred_element_type=jnp.float32)


def tn_dot(a, b):
    return lax.dot_general(a, b, (((0,), (0,)), ((), ())), preferred_element_type=jnp.float32)


def nn_dot(a, b):
    return jnp.dot(a, b, preferred_element_type=jnp.float32)


def split_three(x):
    high = x.astype(jnp.bfloat16)
    rest = x - high.astype(jnp.float32)
    middle = rest.astype(jnp.bfloat16)
    low = (rest - middle.astype(jnp.float32)).astype(jnp.bfloat16)
    return high, middle, low


def smoother_kernel(
    n_dom, x_hbm, lw_hbm, w_hbm, p_hbm, smoothed_ref, score_ref,
    lw_ref, w_ref, p_ref, held, kernel_rows, stats, inverse_norm, bias, weights, stage, in_sem, send_sem, recv_sem,
):
    rows, width = x_hbm.shape[1:]
    total = n_dom * rows
    steps = 4
    half = total // 2
    dom = lax.axis_index("dom")
    tm = lax.axis_index("tm")
    group, side = dom // 2, dom % 2
    high, low = group // 2, group % 2
    near = 2 * high + 1 - low
    mirror = 2 * (1 - high) + low
    opposite = 2 * (1 - high) + 1 - low
    across = dom + 1 - 2 * side
    other = 1 - tm
    mine = tm * n_dom + group
    peers = [2 * g + side for g in (near, mirror, opposite)]

    loads = [
        pltpu.make_async_copy(source, target, in_sem.at[i])
        for i, (source, target) in enumerate(
            [
                (w_hbm, w_ref),
                (p_hbm, p_ref),
                (lw_hbm, lw_ref),
                (x_hbm.at[0], held.at[mine, 0:rows]),
                (x_hbm.at[1], held.at[mine, rows : 2 * rows]),
            ]
        )
    ]
    for load in loads:
        load.start()

    barrier = pltpu.get_barrier_semaphore()
    targets = [(peer, tm) for peer in peers] + [(across, tm), (dom, other)]
    for to_dom, to_tm in targets:
        pl.semaphore_signal(
            barrier, inc=1, device_id={"dom": to_dom, "tm": to_tm}, device_id_type=MESH
        )

    for load in loads:
        load.wait()
    weight = w_ref[...]
    p_row = p_ref[...]
    p_down = jnp.broadcast_to(p_row, (width, width)).T
    stage[...] = jnp.zeros_like(stage)
    terms = []
    for k in range(2):
        x_k = held[mine, k * rows : (k + 1) * rows, :]
        predicted = nt_dot(weight, x_k)
        energy = jnp.sum(p_down[:, :rows] * predicted * predicted, axis=0, keepdims=True)
        terms.append(lw_ref[k : k + 1, :] - 0.5 * energy)
    terms.append(lw_ref[1:2, :])
    for q in range(3):
        for piece, value in enumerate(split_three(terms[q])):
            row = 3 * piece + q
            stage[row : row + 1, 0:rows] = value.astype(jnp.float32)
    held[mine, 2 * rows : 2 * rows + EXTRA, :] = stage[...].astype(jnp.bfloat16)

    pl.semaphore_wait(barrier, len(targets))

    sends = []

    def transfer(source, target, index, to_dom, to_tm):
        return pltpu.make_async_remote_copy(
            src_ref=held.at[source],
            dst_ref=held.at[target],
            send_sem=send_sem.at[index],
            recv_sem=recv_sem.at[target],
            device_id={"dom": to_dom, "tm": to_tm},
            device_id_type=MESH,
        )

    def send(source, target, to_dom, to_tm):
        copy = transfer(source, target, len(sends), to_dom, to_tm)
        copy.start()
        sends.append(copy)

    def arrive(slot):
        transfer(slot, slot, 0, dom, other).wait_recv()

    base, far_base = tm * n_dom, other * n_dom
    part = n_dom // 2
    for peer in peers:
        send(mine, mine, peer, tm)
    send(mine, mine + part, across, tm)
    send(mine, mine, dom, other)

    scaled = jnp.concatenate(split_three(p_down * weight.astype(jnp.float32)), axis=1)
    line = lax.broadcasted_iota(jnp.int32, (EXTRA, 3 * width), 0)
    which = lax.broadcasted_iota(jnp.int32, (EXTRA, 3 * width), 1) // width
    pick = jnp.where((line < 9) & (line % 3 == which), 1.0, 0.0).astype(jnp.bfloat16)

    def set_of(at, k):
        return held[pl.ds(at, part), k * rows : (k + 1) * rows, :].reshape(half, width)

    def spread_bias(h):
        for c in range(2):
            for g in range(part):
                s = c * n_dom + h * part + g
                spread = tn_dot(held[s, 2 * rows : 2 * rows + EXTRA, :], pick)
                for k in range(2):
                    t = 2 * c + k
                    q = 2 if t == steps - 1 else k
                    bias[t, h, g * rows : (g + 1) * rows, :] = spread[:rows, q * width : (q + 1) * width]

    def tile(t, column_at, column_k, row_at, row_k, j, i):
        wide = nn_dot(set_of(row_at + i * part, row_k), scaled)
        projected = (
            wide[:, :width] + (wide[:, width : 2 * width] + wide[:, 2 * width :])
        ).astype(jnp.bfloat16)
        scores = nt_dot(set_of(column_at + j * part, column_k), projected)
        scores = scores + jnp.concatenate([bias[t, j]] * (half // width), axis=1)
        top = jnp.max(scores, axis=0, keepdims=True)
        terms = jnp.exp(scores - top)
        kernel_rows[t, j, :, i * half : (i + 1) * half] = terms.astype(jnp.bfloat16)
        stats[t, 2 * j + i, 0:1, :] = top
        stats[t, 2 * j + i, 1:2, :] = jnp.sum(terms, axis=0, keepdims=True)

    def tall_tile(t, column_at, column_k, row_at, row_k):
        wide = nn_dot(set_of(row_at + part, row_k), scaled)
        projected = (
            wide[:, :width] + (wide[:, width : 2 * width] + wide[:, 2 * width :])
        ).astype(jnp.bfloat16)
        columns = [set_of(column_at + j * part, column_k) for j in range(2)]
        scores = nt_dot(jnp.concatenate(columns, axis=0), projected)
        column_bias = bias[t].reshape(total, width)
        scores = scores + jnp.concatenate([column_bias] * (half // width), axis=1)
        top = jnp.max(scores, axis=0, keepdims=True)
        terms = jnp.exp(scores - top)
        rounded = terms.astype(jnp.bfloat16)
        stats[t, 1, 1:2, :] = jnp.sum(terms, axis=0, keepdims=True)
        for j in range(2):
            kernel_rows[t, j, :, half:] = rounded[j * half : (j + 1) * half]

    own_t = (2 * tm, base, 0, base, 1)
    middle_t = (1, 0, 1, n_dom, 0)
    other_t = (2 * other, far_base, 0, far_base, 1)

    for n, g in enumerate((near, mirror, opposite)):
        arrive(base + g)
        send(base + g, base + g + part, across, tm)
        send(base + g, base + g, dom, other)
        if n == 0:
            arrive(base + part + group)
            send(base + part + group, base + part + group, dom, other)
    for g in range(part):
        arrive(far_base + g)
    spread_bias(0)
    for case in (own_t, middle_t, other_t):
        tile(*case, 0, 0)
    for g in (near, mirror, opposite):
        arrive(base + part + g)
        send(base + part + g, base + part + g, dom, other)
    for g in range(part):
        arrive(far_base + part + g)
    spread_bias(1)

    last = bias[steps - 1].reshape(total, width)
    last = jnp.exp(last - jnp.max(last, axis=0, keepdims=True))
    weights[steps - 1] = last / jnp.sum(last, axis=0, keepdims=True)

    for case in (own_t, middle_t, other_t):
        tile(*case, 1, 0)
        tall_tile(*case)

    score = jnp.zeros((width, width), jnp.float32)
    for t in range(steps - 2, -1, -1):
        tops = [stats[t, 2 * j, 0:1, :] for j in range(2)]
        top = jnp.maximum(tops[0], tops[1])
        scales = [jnp.exp(tops[j] - top) for j in range(2)]
        norm = sum(scales[j] * stats[t, 2 * j, 1:2, :] for j in range(2))
        inverses = [(0, 0, scales[0] / norm), (1, 0, scales[1] / norm)]
        inverses.append((0, half, 1.0 / stats[t, 1, 1:2, :]))
        for j, start, inverse in inverses:
            for b in range(half // width):
                at = start + b * width
                inverse_norm[t, j, at : at + width, :] = jnp.broadcast_to(
                    inverse[:, b * width : (b + 1) * width], (width, width)
                ).T
    for t in range(steps - 2, -1, -1):
        at, k = (t // 2) * n_dom, t % 2
        later_at, later_k = ((t + 1) // 2) * n_dom, (t + 1) % 2
        later = [set_of(later_at + i * part, later_k).astype(jnp.float32) for i in range(2)]

        def weighted(i, j):
            span = slice(i * half, (i + 1) * half)
            ratio = weights[t + 1, span, :] * inverse_norm[t, j, span, :]
            return jnp.concatenate(
                [(ratio * later[i]).astype(jnp.bfloat16), ratio.astype(jnp.bfloat16)], axis=1
            )

        far_right = weighted(1, 0)
        for j in range(2):
            right = jnp.concatenate([weighted(0, j), far_right], axis=0)
            both = nn_dot(kernel_rows[t, j], right)
            now = both[:, width:]
            weights[t, j * half : (j + 1) * half, :] = now
            columns = set_of(at + j * part, k)
            predicted = nt_dot(columns, weight)
            residual = (both[:, :width] - predicted * now).astype(jnp.bfloat16)
            score = score + tn_dot(residual, columns)
    score_ref[...] = score * p_down
    first = pl.multiple_of(group * rows, rows)
    for k in range(2):
        own = weights[2 * tm + k, pl.ds(first, rows), :]
        smoothed_ref[k : k + 1, :] = own.T[0:1, :] * total
    for copy in sends:
        copy.wait_send()


def hand_over(a_in, b_in, a_out, b_out, a_held, b_held, sems):
    arriving = [
        pltpu.make_async_copy(a_in, a_held, sems.at[0]),
        pltpu.make_async_copy(b_in, b_held, sems.at[1]),
    ]
    leaving = [
        pltpu.make_async_copy(a_held, a_out, sems.at[2]),
        pltpu.make_async_copy(b_held, b_out, sems.at[3]),
    ]
    for copy in arriving:
        copy.start()
    for first, then in zip(arriving, leaving):
        first.wait()
        then.start()
    for copy in leaving:
        copy.wait()


def fused(particles, log_weight, trans_weight, precision):
    steps_here, rows, width = particles.shape
    n_dom = lax.axis_size("dom")
    total = n_dom * rows
    whole = pl.BlockSpec(memory_space=pltpu.VMEM)
    copies = (n_dom // 2 - 1) * 3 + 2 + n_dom // 2
    smoothed, score = pl.pallas_call(
        functools.partial(smoother_kernel, n_dom),
        out_shape=(
            jax.ShapeDtypeStruct((steps_here, rows), jnp.float32),
            jax.ShapeDtypeStruct((width, width), jnp.float32),
        ),
        in_specs=[pl.BlockSpec(memory_space=pltpu.HBM)] * 4,
        out_specs=(whole, whole),
        scratch_shapes=[
            pltpu.VMEM((steps_here, rows), jnp.float32),
            pltpu.VMEM((width, width), jnp.bfloat16),
            pltpu.VMEM((1, width), jnp.float32),
            pltpu.VMEM((2 * n_dom, 2 * rows + EXTRA, width), jnp.bfloat16),
            pltpu.VMEM((3, 2, total // 2, total), jnp.bfloat16),
            pltpu.VMEM((3, 4, 8, total // 2), jnp.float32),
            pltpu.VMEM((3, 2, total, width), jnp.float32),
            pltpu.VMEM((4, 2, total // 2, width), jnp.float32),
            pltpu.VMEM((4, total, width), jnp.float32),
            pltpu.VMEM((EXTRA, width), jnp.float32),
            pltpu.SemaphoreType.DMA((5,)),
            pltpu.SemaphoreType.DMA((copies,)),
            pltpu.SemaphoreType.DMA((2 * n_dom,)),
        ],
        compiler_params=pltpu.CompilerParams(
            collective_id=0, has_side_effects=True, vmem_limit_bytes=64 * 2**20
        ),
    )(particles, log_weight, trans_weight, precision.reshape(1, width))
    return pl.pallas_call(
        hand_over,
        out_shape=(
            jax.ShapeDtypeStruct((steps_here, rows), jnp.float32),
            jax.ShapeDtypeStruct((width, width), jnp.float32),
        ),
        in_specs=[pl.BlockSpec(memory_space=pltpu.HBM)] * 2,
        out_specs=(pl.BlockSpec(memory_space=pltpu.HBM),) * 2,
        scratch_shapes=[
            pltpu.VMEM((steps_here, rows), jnp.float32),
            pltpu.VMEM((width, width), jnp.float32),
            pltpu.SemaphoreType.DMA((4,)),
        ],
        compiler_params=pltpu.CompilerParams(vmem_limit_bytes=64 * 2**20),
    )(smoothed, score)


def plan(particles, log_weight, trans_weight, precision):
    steps_here, rows, width = particles.shape
    n_dom = lax.axis_size("dom")
    total = n_dom * rows
    small = total <= MOST_ROWS and total % (2 * width) == 0 and rows <= width and rows % 16 == 0
    shaped = n_dom == 8 and lax.axis_size("tm") == 2 and steps_here == 2 and width == 128
    if small and shaped:
        return fused(particles, log_weight, trans_weight, precision)
    return shards(particles, log_weight, trans_weight, precision)


def solution(mesh):
    placed = (P("tm", ("seq", "dom"), None), P("tm", ("seq", "dom")), P(), P())
    return jax.shard_map(
        plan,
        mesh=mesh,
        in_specs=placed,
        out_specs=(P("tm", ("seq", "dom")), P("seq", None)),
        check_vma=False,
    )
```
